32 devices in a mesh: sect: 4 (over x, core), batch: 8 (over z, y).
Axes of the slice: x: 2, y: 2, z: 4, core: 2. Of those that a mesh axis runs over, the one named last changes fastest.
Arguments:
- warm: bfloat16 [8192, 640], P(('sect', 'batch')), may hold values from -6 to 6
- latents: float32 [4, 1024], P(None, 'batch'), may hold values from -6 to 6
- timesteps: int32 [5], replicated, may hold values from 300 to 599
- assign: int32 [8], P('batch'), may hold values from 0 to 7, each once
- prompts: bfloat16 [8, 640], P('batch'), may hold values from -6 to 6
- w_in: bfloat16 [2560, 2560], P('sect'), may hold values from -0.25 to 0.25
- time_w: bfloat16 [2560, 640], P('sect'), may hold values from -0.25 to 0.25
- w_out: bfloat16 [5120, 640], P(('sect', 'batch')), may hold values from -0.15625 to 0.15625
- conv_in_w: bfloat16 [4, 640], replicated, may hold values from -3 to 3
- conv_out_w: bfloat16 [4, 640], replicated, may hold values from -0.25 to 0.25
Outputs:
- segments: bfloat16 [8192, 640], P(('sect', 'batch'))
- final_latents: float32 [4, 1024], P('sect', 'batch')
The draws below stay inside these ranges and needn't reach their ends.
Inputs may be any that keep to these rules, and one draw needn't show every extreme that they name: `assign`: each prompt is assigned to exactly one prompt batch.
All inputs are finite; a program needn't handle non-finite values.
Results may differ from the reference program's by a relative error of at most 0.015.
Values may be sent and summed in bfloat16 or wider, within the bound.
A program may use at most 64 MiB of HBM per device.

```python
import math
import jax
import jax.numpy as jnp
from jax import lax

C = 640
FFI = 1280
LAT = 4
P_SIZE = 128
STEPS = 4
PROMPTS = 8
LAT_COLS = 1024
SEGMENT_ROWS = 8192
N_SECT = 4
N_BATCH = 8


def with_ends(entries, key, least, top_value):
    longest = entries.shape.index(max(entries.shape))
    spots = []
    for shift in (0, 1):
        where = [jax.random.randint(jax.random.fold_in(key, axis), (), 0, length) for axis, length in enumerate(entries.shape)]
        where[longest] = (where[longest] + shift) % entries.shape[longest]
        spots.append(tuple(where))
    return entries.at[spots[0]].set(least).at[spots[1]].set(top_value)


def level_of(own_key, dims, pieces, smallest, top_value):
    loudness, own = 1.0, jax.random.fold_in(own_key, 6)
    for dim, blocks in pieces:
        heights = jnp.exp(jax.random.uniform(jax.random.fold_in(own, dim), (blocks,), jnp.float32, smallest / len(pieces), top_value / len(pieces)))
        loudness = loudness * jnp.repeat(heights, dims[dim] // blocks).reshape([-1 if axis == dim else 1 for axis in range(len(dims))])
    return loudness


def bell_draw(key, extent, deviation, most, shards=(), held_as=jnp.bfloat16):
    level = level_of(key, extent, shards, -0.22, 0.18) if shards else 1.0
    result = jax.random.normal(key, extent, jnp.float32) * deviation * level
    return jnp.minimum(jnp.maximum(result, -most), most).astype(held_as)


def setup_inputs(seed: int = 0) -> dict:
    splits = jax.random.split(jax.random.key(seed), 11)
    warm = bell_draw(splits[0], (SEGMENT_ROWS, C), 1.0, 6.0, ((0, 32),))
    latents = bell_draw(splits[1], (LAT, LAT_COLS), 1.0, 6.0, ((1, 8),), jnp.float32)
    timesteps = with_ends(jax.random.randint(splits[2], (STEPS + 1,), 300, 600), jax.random.fold_in(splits[2], 1), 300, 599).astype(jnp.int32)
    assign = jax.random.permutation(splits[3], PROMPTS).astype(jnp.int32)
    prompts = bell_draw(splits[4], (PROMPTS, C), 1.0, 6.0, ((0, 8),))
    w_in = bell_draw(splits[5], (N_SECT * C, 2 * FFI), C ** -0.5, 0.25, ((0, 4),))
    time_w = bell_draw(splits[6], (N_SECT * C, C), C ** -0.5, 0.25, ((0, 4),))
    w_out = bell_draw(splits[7], (N_SECT * FFI, C), FFI ** -0.5, 0.15625, ((0, 32),))
    conv_in_w = bell_draw(splits[8], (LAT, C), LAT ** -0.5, 3.0)
    conv_out_w = bell_draw(splits[9], (LAT, C), C ** -0.5, 0.25)
    return {"warm": warm, "latents": latents, "timesteps": timesteps, "assign": assign, "prompts": prompts, "w_in": w_in, "time_w": time_w, "w_out": w_out, "conv_in_w": conv_in_w, "conv_out_w": conv_out_w}


guidance_scale = 3.0

def sinusoid(time_value, channels):
    half_width = channels // 2
    frequency = jnp.exp(-math.log(10000.0) * jnp.arange(half_width, dtype=jnp.float32) / half_width)
    angles = time_value.astype(jnp.float32) * frequency
    return jnp.concatenate([jnp.cos(angles), jnp.sin(angles)])

def alpha_bar(time_value):
    phase_angle = (time_value.astype(jnp.float32) / 1000.0 + 0.008) / 1.008 * (math.pi / 2)
    return jnp.cos(phase_angle) ** 2

def rms_norm(values):
    return values * lax.rsqrt(lax.optimization_barrier(jnp.mean(values * values, axis=-1, keepdims=True)) + 1e-06)

def feed_block(inputs, time_vec, cond_rows, weight_in, weight_out, hidden_units):
    summed = inputs + time_vec + cond_rows
    normed = rms_norm(summed).astype(jnp.bfloat16)
    projected = jnp.dot(normed, weight_in, preferred_element_type=jnp.float32)
    hidden = (projected[:, :hidden_units] * jax.nn.gelu(projected[:, hidden_units:], approximate=False)).astype(jnp.bfloat16)
    return (summed + jnp.dot(hidden, weight_out, preferred_element_type=jnp.float32)).astype(jnp.bfloat16)

def reference(warm, latents, timesteps, assign, prompts, w_in, time_w, w_out, conv_in_w, conv_out_w):
    rows = 2 * P_SIZE
    whole = N_BATCH * rows
    segment_list = [warm[section * whole:(section + 1) * whole] for section in range(N_SECT)]
    chosen = prompts[assign].astype(jnp.float32)
    cond = jnp.concatenate([jnp.broadcast_to(chosen[:, None, :], (N_BATCH, P_SIZE, C)), jnp.zeros((N_BATCH, P_SIZE, C), jnp.float32)], axis=1).reshape(whole, C)
    latent = latents
    for step_index in range(STEPS):
        time_now = timesteps[step_index]
        time_next = timesteps[step_index + 1]
        embedded = jax.nn.silu(sinusoid(time_now, C)).astype(jnp.bfloat16)
        latent_bf = latent.astype(jnp.bfloat16).astype(jnp.float32).reshape(LAT, N_BATCH, P_SIZE)
        first = jnp.einsum('lbp,lc->bpc', latent_bf, conv_in_w.astype(jnp.float32)).astype(jnp.bfloat16)
        first = jnp.concatenate([first, first], axis=1).reshape(whole, C)
        new_list = []
        for section in range(N_SECT):
            if section == 0:
                inputs = first.astype(jnp.float32)
            else:
                inputs = segment_list[section - 1].astype(jnp.float32)
            skip_rows = segment_list[(section + 1) % N_SECT].astype(jnp.float32)
            inputs = (inputs + skip_rows) * 0.5
            time_vec = jnp.dot(embedded[None, :], time_w[section * C:(section + 1) * C], preferred_element_type=jnp.float32)
            new_list.append(feed_block(inputs, time_vec, cond, w_in[section * C:(section + 1) * C], w_out[section * FFI:(section + 1) * FFI], FFI))
        final_segment = new_list[-1]
        activated = jax.nn.silu(rms_norm(final_segment.astype(jnp.float32))).astype(jnp.bfloat16)
        noise = jnp.einsum('lc,bqc->lbq', conv_out_w.astype(jnp.float32), activated.astype(jnp.float32).reshape(N_BATCH, rows, C))
        guided = noise[:, :, P_SIZE:] + guidance_scale * (noise[:, :, :P_SIZE] - noise[:, :, P_SIZE:])
        guided = guided.reshape(LAT, N_BATCH * P_SIZE)
        bar_now = alpha_bar(time_now)
        bar_next = alpha_bar(time_next)
        clean = (latent - jnp.sqrt(1.0 - bar_now) * guided) / jnp.sqrt(bar_now)
        latent = jnp.sqrt(bar_next) * clean + jnp.sqrt(1.0 - bar_next) * guided
        segment_list = new_list
    return (jnp.concatenate(segment_list, axis=0), latent)
```

```python
import functools
import math

import jax
import jax.numpy as jnp
from jax import lax
from jax.experimental import pallas as pl
from jax.experimental.pallas import tpu as pltpu
from jax.sharding import PartitionSpec as P

guidance_scale = 3.0
MESH = pl.DeviceIdType.MESH
F32 = jnp.float32
BF16 = jnp.bfloat16
CHUNKS = 2


def kernel(
    sects, batches, gathered,
    ts_ref, assign_ref, warm_ref, lat_ref, prompts_ref, w_in_ref, time_w_ref, w_out_ref, cin_ref, cout_ref,
    oseg_ref, olat_ref,
    w_in, time_w, w_all, xbuf, kbuf, ybuf, a_scr, h_scr, tv, roots, rests, cond, ptab, pown,
    cin, cout, lat, latin, latout, fin, fin_in,
    load_sem, x_send, x_recv, k_send, k_recv, l_send, l_recv, f_send, f_recv,
    p_send, p_recv, g_line, g_side, g_recv,
):
    s = lax.axis_index("sect")
    me = lax.axis_index("batch")
    steps = ts_ref.shape[0] - 1
    _, positions, channels = warm_ref.shape
    hidden = w_all.shape[0]
    part = positions // CHUNKS
    up = lax.rem(s + 1, sects)
    down = lax.rem(s + sects - 1, sects)
    last = sects - 1

    loads = [
        pltpu.make_async_copy(time_w_ref, time_w, load_sem.at[0]),
        pltpu.make_async_copy(w_in_ref, w_in, load_sem.at[1]),
    ]
    if gathered:
        loads.append(pltpu.make_async_copy(w_out_ref, w_all, load_sem.at[2]))
    else:
        depth = w_out_ref.shape[0]
        own_rows = pl.ds(pl.multiple_of(me * depth, depth), depth)
        loads.append(pltpu.make_async_copy(w_out_ref, w_all.at[own_rows], load_sem.at[2]))
    for copy in loads:
        copy.start()

    barrier = pltpu.get_barrier_semaphore()
    for d in range(1, sects):
        pl.semaphore_signal(barrier, inc=1, device_id={"sect": lax.rem(s + d, sects)}, device_id_type=MESH)
    met = sects - 1
    if not gathered:
        for d in range(1, batches):
            pl.semaphore_signal(barrier, inc=1, device_id={"batch": lax.rem(me + d, batches)}, device_id_type=MESH)
        met += batches - 1
        pown[...] = prompts_ref[...].astype(F32)
    pl.semaphore_wait(barrier, met)

    def rows(c):
        return pl.ds(c * part, part)

    def x_copy(src, slot, c):
        return pltpu.make_async_remote_copy(
            src_ref=src, dst_ref=xbuf.at[slot, :, rows(c), :], send_sem=x_send.at[slot, c],
            recv_sem=x_recv.at[slot, c], device_id={"sect": up}, device_id_type=MESH)

    def k_copy(src, slot, c):
        return pltpu.make_async_remote_copy(
            src_ref=src, dst_ref=kbuf.at[slot, :, rows(c), :], send_sem=k_send.at[slot, c],
            recv_sem=k_recv.at[slot, c], device_id={"sect": down}, device_id_type=MESH)

    def l_copy(slot, c):
        return pltpu.make_async_remote_copy(
            src_ref=latout.at[slot, rows(c), :], dst_ref=latin.at[slot, rows(c), :], send_sem=l_send.at[slot, c],
            recv_sem=l_recv.at[slot, c], device_id={"sect": 0}, device_id_type=MESH)

    def f_copy(d):
        return pltpu.make_async_remote_copy(
            src_ref=fin.at[d], dst_ref=fin_in, send_sem=f_send.at[d],
            recv_sem=f_recv, device_id={"sect": d}, device_id_type=MESH)

    if not gathered:
        z, y = me // 2, lax.rem(me, 2)
        length = batches // 2
        side = z * 2 + (1 - y)

        def p_copy(d):
            return pltpu.make_async_remote_copy(
                src_ref=pown, dst_ref=ptab.at[me], send_sem=p_send.at[d], recv_sem=p_recv.at[me],
                device_id={"batch": lax.rem(me + d, batches)}, device_id_type=MESH)

        def block(b):
            return w_all.at[pl.ds(pl.multiple_of(b * depth, depth), depth)]

        def g_copy(b, to, sems, src=None):
            return pltpu.make_async_remote_copy(
                src_ref=block(b) if src is None else src, dst_ref=block(b), send_sem=sems.at[b],
                recv_sem=g_recv.at[b], device_id={"batch": to}, device_id_type=MESH)

        def g_arrived(b):
            pltpu.make_async_copy(block(b), block(b), g_recv.at[b]).wait()

        for d in range(1, batches):
            p_copy(d).start()

        @pl.when(z < length - 1)
        def _():
            g_copy(me, me + 2, g_line.at[0], w_out_ref).start()

        @pl.when(z > 0)
        def _():
            g_copy(me, me - 2, g_line.at[1], w_out_ref).start()

        g_copy(me, side, g_side, w_out_ref).start()

    for c in range(CHUNKS):
        @pl.when(s < last)
        def _(c=c):
            x_copy(warm_ref.at[:, rows(c), :], 0, c).start()
        k_copy(warm_ref.at[:, rows(c), :], 0, c).start()

    cin[...] = jnp.zeros_like(cin)
    cout[...] = jnp.zeros_like(cout)
    levels = cin_ref.shape[0]
    cin[0:levels, :] = cin_ref[...].astype(F32)
    cout[0:levels, :] = cout_ref[...].astype(F32)
    lat[...] = jnp.zeros_like(lat)
    lat[0:levels, :] = lat_ref[...]
    turned = lat[...].T
    lat[...] = turned
    latin[0] = turned.astype(BF16)
    which = lax.broadcasted_iota(jnp.int32, (16, 128), 0)
    times = jnp.zeros((16, 128), F32)
    for i in range(steps + 1):
        times = jnp.where(which == i, ts_ref[i].astype(F32), times)
    bar = jnp.cos((times / 1000.0 + 0.008) / 1.008 * (math.pi / 2)) ** 2
    roots[...] = jnp.sqrt(bar)
    rests[...] = jnp.sqrt(1.0 - bar)
    half = channels // 2
    lane = lax.broadcasted_iota(jnp.int32, (16, channels), 1)
    wave = jnp.where(lane < half, lane, lane - half).astype(F32)
    frequency = jnp.exp(-math.log(10000.0) * wave / half)
    angles = jnp.concatenate([times] * (channels // 128), axis=1) * frequency
    waves = jnp.where(lane < half, jnp.cos(angles), jnp.sin(angles))
    embedded = (waves * (1.0 / (1.0 + jnp.exp(-waves)))).astype(BF16)
    loads[0].wait()
    tv[...] = jnp.dot(embedded, time_w[...], preferred_element_type=F32)

    if gathered:
        cond[...] = prompts_ref[...]
    else:
        ptab[me] = pown[...]
        for d in range(1, batches):
            b = lax.rem(me + d, batches)
            pltpu.make_async_copy(ptab.at[b], ptab.at[b], p_recv.at[b]).wait()
        cond[...] = ptab[assign_ref[0]]

    def front(i, c):
        @pl.when(s == 0)
        def _():
            @pl.when(i > 0)
            def _():
                l_copy(i, c).wait_recv()
            first = jnp.dot(latin[i, rows(c), :], cin[...].astype(BF16), preferred_element_type=F32).astype(BF16)
            xbuf[i, 0, rows(c), :] = first
            xbuf[i, 1, rows(c), :] = first

        @pl.when(s > 0)
        def _():
            x_copy(ybuf.at[i, :, rows(c), :], i, c).wait_recv()

        k_copy(ybuf.at[i, :, rows(c), :], i, c).wait_recv()
        time_vec = tv[pl.ds(i, 1), :]
        for g in range(2):
            a = 0.5 * (xbuf[i, g, rows(c), :].astype(F32) + kbuf[i, g, rows(c), :].astype(F32)) + time_vec
            if g == 0:
                a = a + cond[...]
            a_scr[c, g * part:(g + 1) * part, :] = a
        a = a_scr[c]
        normed = (a * lax.rsqrt(jnp.mean(a * a, axis=-1, keepdims=True) + 1e-6)).astype(BF16)
        tile = 256 if hidden % 256 == 0 else hidden
        for j in range(0, hidden, tile):
            gate = jnp.dot(normed, w_in[:, hidden + j:hidden + j + tile], preferred_element_type=F32)
            value = jnp.dot(normed, w_in[:, j:j + tile], preferred_element_type=F32)
            gelu = 0.5 * gate * (1.0 + lax.erf(gate * math.sqrt(0.5)))
            h_scr[c, :, j:j + tile] = (value * gelu).astype(BF16)

    def back(i, c):
        out = (a_scr[c] + jnp.dot(h_scr[c], w_all[...], preferred_element_type=F32)).astype(BF16)

        @pl.when(i < steps - 1)
        def _():
            ybuf[i + 1, :, rows(c), :] = out.reshape(2, part, channels)

            @pl.when(s < last)
            def _():
                x_copy(ybuf.at[i + 1, :, rows(c), :], i + 1, c).start()
            k_copy(ybuf.at[i + 1, :, rows(c), :], i + 1, c).start()

        @pl.when(i == steps - 1)
        def _():
            oseg_ref[:, rows(c), :] = out.reshape(2, part, channels)

        @pl.when(s == last)
        def _():
            v = out.astype(F32)
            v = v * lax.rsqrt(jnp.mean(v * v, axis=-1, keepdims=True) + 1e-6)
            m = (v * (1.0 / (1.0 + jnp.exp(-v)))).astype(BF16)
            e = lax.dot_general(m, cout[...].astype(BF16), (((1,), (1,)), ((), ())), preferred_element_type=F32)
            guided = e[part:] + guidance_scale * (e[:part] - e[part:])
            root_now, root_next = roots[pl.ds(i, 1), :], roots[pl.ds(i + 1, 1), :]
            rest_now, rest_next = rests[pl.ds(i, 1), :], rests[pl.ds(i + 1, 1), :]
            clean = (lat[rows(c), :] - rest_now * guided) / root_now
            new = root_next * clean + rest_next * guided
            lat[rows(c), :] = new

            @pl.when(i < steps - 1)
            def _():
                latout[i + 1, rows(c), :] = new.astype(BF16)
                l_copy(i + 1, c).start()

    def pass_on(k):
        @pl.when(z >= k)
        def _():
            b = me - 2 * k
            g_arrived(b)

            @pl.when(z < length - 1)
            def _():
                g_copy(b, me + 2, g_line.at[0]).start()
            g_copy(b, side, g_side).start()

        @pl.when(z + k < length)
        def _():
            b = me + 2 * k
            g_arrived(b)

            @pl.when(z > 0)
            def _():
                g_copy(b, me - 2, g_line.at[1]).start()
            g_copy(b, side, g_side).start()

    if not gathered:
        pass_on(1)
    loads[1].wait()
    for c in range(CHUNKS):
        front(0, c)
    loads[2].wait()
    if not gathered:
        for k in range(2, length):
            pass_on(k)
        for k in range(length):
            g_arrived(2 * k + (1 - y))
    for c in range(CHUNKS):
        back(0, c)

    def body(i, carry):
        for c in range(CHUNKS):
            front(i, c)
            back(i, c)
        return carry

    lax.fori_loop(1, steps, body, 0)

    @pl.when(s == last)
    def _():
        turned = lat[...].T
        here = olat_ref.shape[0]
        for d in range(sects):
            fin[d] = turned[d * here:(d + 1) * here, :]
        for d in range(sects - 1):
            f_copy(d).start()
        olat_ref[...] = fin[last]
        for d in range(sects - 1):
            f_copy(d).wait_send()
        for i in range(1, steps):
            for c in range(CHUNKS):
                l_copy(i, c).wait_send()

    @pl.when(s < last)
    def _():
        f_copy(0).wait_recv()
        olat_ref[...] = fin_in[...]
        for i in range(steps):
            for c in range(CHUNKS):
                x_copy(ybuf.at[i, :, rows(c), :], i, c).wait_send()

    for i in range(steps):
        for c in range(CHUNKS):
            k_copy(ybuf.at[i, :, rows(c), :], i, c).wait_send()
    if not gathered:
        for d in range(1, batches):
            p_copy(d).wait_send()
        for k in range(length):
            @pl.when(z >= k)
            def _(k=k):
                b = me - 2 * k

                @pl.when(z < length - 1)
                def _():
                    g_copy(b, me + 2, g_line.at[0]).wait_send()
                g_copy(b, side, g_side).wait_send()

            @pl.when(z + k < length)
            def _(k=k):
                b = me + 2 * k

                @pl.when(z > 0)
                def _():
                    g_copy(b, me - 2, g_line.at[1]).wait_send()
                if k > 0:
                    g_copy(b, side, g_side).wait_send()


def on_device(
    sects, batches, warm, latents, timesteps, assign, prompts, w_in, time_w, w_out, conv_in_w, conv_out_w
):
    positions = latents.shape[1]
    channels = warm.shape[1]
    hidden = w_out.shape[0] * batches
    steps = timesteps.shape[0] - 1
    gathered = w_out.shape[0] % 16 != 0 or batches % 2 != 0
    if gathered:
        w_out = lax.all_gather(w_out, "batch", axis=0, tiled=True)
        table = lax.all_gather(prompts, "batch", axis=0, tiled=True)
        prompts = lax.dynamic_slice_in_dim(table, assign[0], 1, 0).astype(F32)
    whole = pl.BlockSpec(memory_space=pltpu.VMEM)
    apart = pl.BlockSpec(memory_space=pl.ANY)
    scalars = pl.BlockSpec(memory_space=pltpu.SMEM)
    here = latents.shape[0] // sects
    dma = pltpu.SemaphoreType.DMA
    width = 2 * positions // CHUNKS
    segment, final = pl.pallas_call(
        functools.partial(kernel, sects, batches, gathered),
        out_shape=(
            jax.ShapeDtypeStruct((2, positions, channels), BF16),
            jax.ShapeDtypeStruct((here, positions), F32),
        ),
        in_specs=[scalars, scalars, apart, whole, whole, apart, apart, apart, whole, whole],
        out_specs=(whole, whole),
        scratch_shapes=[
            pltpu.VMEM(w_in.shape, BF16),
            pltpu.VMEM(time_w.shape, BF16),
            pltpu.VMEM((hidden, channels), BF16),
            pltpu.VMEM((steps, 2, positions, channels), BF16),
            pltpu.VMEM((steps, 2, positions, channels), BF16),
            pltpu.VMEM((steps, 2, positions, channels), BF16),
            pltpu.VMEM((CHUNKS, width, channels), F32),
            pltpu.VMEM((CHUNKS, width, hidden), BF16),
            pltpu.VMEM((16, channels), F32),
            pltpu.VMEM((16, 128), F32),
            pltpu.VMEM((16, 128), F32),
            pltpu.VMEM((1, channels), F32),
            pltpu.VMEM((batches, 1, channels), F32),
            pltpu.VMEM((1, channels), F32),
            pltpu.VMEM((128, channels), F32),
            pltpu.VMEM((128, channels), F32),
            pltpu.VMEM((128, positions), F32),
            pltpu.VMEM((steps, positions, 128), BF16),
            pltpu.VMEM((steps, positions, 128), BF16),
            pltpu.VMEM((sects, here, positions), F32),
            pltpu.VMEM((here, positions), F32),
            dma((3,)),
            dma((steps, CHUNKS)), dma((steps, CHUNKS)),
            dma((steps, CHUNKS)), dma((steps, CHUNKS)),
            dma((steps, CHUNKS)), dma((steps, CHUNKS)),
            dma((sects,)), dma(()),
            dma((batches,)), dma((batches,)),
            dma((2, batches)), dma((batches,)), dma((batches,)),
        ],
        compiler_params=pltpu.CompilerParams(
            collective_id=0, has_side_effects=True, vmem_limit_bytes=40 * 1024 * 1024
        ),
    )(
        timesteps, assign, warm.reshape(2, positions, channels), latents, prompts,
        w_in, time_w, w_out, conv_in_w, conv_out_w,
    )
    return segment.reshape(2 * positions, channels), final


def solution(mesh):
    return jax.shard_map(
        functools.partial(on_device, mesh.shape["sect"], mesh.shape["batch"]),
        mesh=mesh,
        in_specs=(
            P(("sect", "batch"), None),
            P(None, "batch"),
            P(),
            P("batch"),
            P("batch", None),
            P("sect", None),
            P("sect", None),
            P(("sect", "batch"), None),
            P(),
            P(),
        ),
        out_specs=(P(("sect", "batch"), None), P("sect", "batch")),
        check_vma=False,
    )
```

```python
import functools
import math

import jax
import jax.numpy as jnp
from jax import lax
from jax.experimental import pallas as pl
from jax.experimental.pallas import tpu as pltpu
from jax.sharding import PartitionSpec as P

guidance_scale = 3.0
MESH = pl.DeviceIdType.MESH
F32 = jnp.float32
BF16 = jnp.bfloat16
CHUNKS = 2


def kernel(
    sects, batches, gathered,
    ts_hbm, assign_hbm, warm_ref, lat_hbm, prompts_hbm, w_in_ref, time_w_ref, w_out_ref, cin_hbm, cout_hbm,
    oseg_ref, olat_ref,
    ts_ref, assign_ref, lat_ref, prompts_ref, cin_ref, cout_ref,
    w_in, time_w, w_all, xbuf, kbuf, ybuf, a_scr, h_scr, tv, roots, rests, cond, ptab, pown,
    cin, cout, lat, latin, latout, fin, fin_in,
    load_sem, x_send, x_recv, k_send, k_recv, l_send, l_recv, f_send, f_recv,
    p_send, p_recv, g_line, g_side, g_recv,
):
    s = lax.axis_index("sect")
    me = lax.axis_index("batch")
    steps = ts_ref.shape[0] - 1
    _, positions, channels = warm_ref.shape
    hidden = w_all.shape[0]
    part = positions // CHUNKS
    up = lax.rem(s + 1, sects)
    down = lax.rem(s + sects - 1, sects)
    last = sects - 1

    loads = [
        pltpu.make_async_copy(time_w_ref, time_w, load_sem.at[0]),
        pltpu.make_async_copy(w_in_ref, w_in, load_sem.at[1]),
    ]
    if gathered:
        loads.append(pltpu.make_async_copy(w_out_ref, w_all, load_sem.at[2]))
    else:
        depth = w_out_ref.shape[0]
        own_rows = pl.ds(pl.multiple_of(me * depth, depth), depth)
        loads.append(pltpu.make_async_copy(w_out_ref, w_all.at[own_rows], load_sem.at[2]))
    pairs = [(prompts_hbm, prompts_ref), (ts_hbm, ts_ref), (assign_hbm, assign_ref), (lat_hbm, lat_ref),
             (cin_hbm, cin_ref), (cout_hbm, cout_ref)]
    for j, (src, dst) in enumerate(pairs):
        loads.append(pltpu.make_async_copy(src, dst, load_sem.at[3 + j]))
    for copy in loads[3:] + loads[:3]:
        copy.start()

    barrier = pltpu.get_barrier_semaphore()
    for d in range(1, sects):
        pl.semaphore_signal(barrier, inc=1, device_id={"sect": lax.rem(s + d, sects)}, device_id_type=MESH)
    met = sects - 1
    if not gathered:
        for d in range(1, batches):
            pl.semaphore_signal(barrier, inc=1, device_id={"batch": lax.rem(me + d, batches)}, device_id_type=MESH)
        met += batches - 1
        loads[3].wait()
        pown[...] = prompts_ref[...].astype(F32)
    pl.semaphore_wait(barrier, met)

    def rows(c):
        return pl.ds(c * part, part)

    def x_copy(src, slot, c):
        return pltpu.make_async_remote_copy(
            src_ref=src, dst_ref=xbuf.at[slot, :, rows(c), :], send_sem=x_send.at[slot, c],
            recv_sem=x_recv.at[slot, c], device_id={"sect": up}, device_id_type=MESH)

    def k_copy(src, slot, c):
        return pltpu.make_async_remote_copy(
            src_ref=src, dst_ref=kbuf.at[slot, :, rows(c), :], send_sem=k_send.at[slot, c],
            recv_sem=k_recv.at[slot, c], device_id={"sect": down}, device_id_type=MESH)

    def l_copy(slot, c):
        return pltpu.make_async_remote_copy(
            src_ref=latout.at[slot, rows(c), :], dst_ref=latin.at[slot, rows(c), :], send_sem=l_send.at[slot, c],
            recv_sem=l_recv.at[slot, c], device_id={"sect": 0}, device_id_type=MESH)

    def f_copy(d):
        return pltpu.make_async_remote_copy(
            src_ref=fin.at[d], dst_ref=fin_in, send_sem=f_send.at[d],
            recv_sem=f_recv, device_id={"sect": d}, device_id_type=MESH)

    if not gathered:
        z, y = me // 2, lax.rem(me, 2)
        length = batches // 2
        side = z * 2 + (1 - y)

        def p_copy(d):
            return pltpu.make_async_remote_copy(
                src_ref=pown, dst_ref=ptab.at[me], send_sem=p_send.at[d], recv_sem=p_recv.at[me],
                device_id={"batch": lax.rem(me + d, batches)}, device_id_type=MESH)

        def block(b):
            return w_all.at[pl.ds(pl.multiple_of(b * depth, depth), depth)]

        def g_copy(b, to, sems, src=None):
            return pltpu.make_async_remote_copy(
                src_ref=block(b) if src is None else src, dst_ref=block(b), send_sem=sems.at[b],
                recv_sem=g_recv.at[b], device_id={"batch": to}, device_id_type=MESH)

        def g_arrived(b):
            pltpu.make_async_copy(block(b), block(b), g_recv.at[b]).wait()

        for d in range(1, batches):
            p_copy(d).start()

        @pl.when(z < length - 1)
        def _():
            g_copy(me, me + 2, g_line.at[0], w_out_ref).start()

        @pl.when(z > 0)
        def _():
            g_copy(me, me - 2, g_line.at[1], w_out_ref).start()

        g_copy(me, side, g_side, w_out_ref).start()

    for c in range(CHUNKS):
        @pl.when(s < last)
        def _(c=c):
            x_copy(warm_ref.at[:, rows(c), :], 0, c).start()
        k_copy(warm_ref.at[:, rows(c), :], 0, c).start()

    if gathered:
        loads[3].wait()
    for copy in loads[4:]:
        copy.wait()
    cin[...] = jnp.zeros_like(cin)
    cout[...] = jnp.zeros_like(cout)
    levels = cin_ref.shape[0]
    cin[0:levels, :] = cin_ref[...].astype(F32)
    cout[0:levels, :] = cout_ref[...].astype(F32)
    lat[...] = jnp.zeros_like(lat)
    lat[0:levels, :] = lat_ref[...]
    turned = lat[...].T
    lat[...] = turned
    latin[0] = turned.astype(BF16)
    which = lax.broadcasted_iota(jnp.int32, (16, 128), 0)
    times = jnp.zeros((16, 128), F32)
    for i in range(steps + 1):
        times = jnp.where(which == i, ts_ref[i].astype(F32), times)
    bar = jnp.cos((times / 1000.0 + 0.008) / 1.008 * (math.pi / 2)) ** 2
    roots[...] = jnp.sqrt(bar)
    rests[...] = jnp.sqrt(1.0 - bar)
    half = channels // 2
    lane = lax.broadcasted_iota(jnp.int32, (16, channels), 1)
    wave = jnp.where(lane < half, lane, lane - half).astype(F32)
    frequency = jnp.exp(-math.log(10000.0) * wave / half)
    angles = jnp.concatenate([times] * (channels // 128), axis=1) * frequency
    waves = jnp.where(lane < half, jnp.cos(angles), jnp.sin(angles))
    embedded = (waves * (1.0 / (1.0 + jnp.exp(-waves)))).astype(BF16)
    loads[0].wait()
    tv[...] = jnp.dot(embedded, time_w[...], preferred_element_type=F32)

    if gathered:
        cond[...] = prompts_ref[...]
    else:
        ptab[me] = pown[...]
        for d in range(1, batches):
            b = lax.rem(me + d, batches)
            pltpu.make_async_copy(ptab.at[b], ptab.at[b], p_recv.at[b]).wait()
        cond[...] = ptab[assign_ref[0]]

    def front(i, c):
        @pl.when(s == 0)
        def _():
            @pl.when(i > 0)
            def _():
                l_copy(i, c).wait_recv()
            first = jnp.dot(latin[i, rows(c), :], cin[...].astype(BF16), preferred_element_type=F32).astype(BF16)
            xbuf[i, 0, rows(c), :] = first
            xbuf[i, 1, rows(c), :] = first

        @pl.when(s > 0)
        def _():
            x_copy(ybuf.at[i, :, rows(c), :], i, c).wait_recv()

        k_copy(ybuf.at[i, :, rows(c), :], i, c).wait_recv()
        time_vec = tv[pl.ds(i, 1), :]
        for g in range(2):
            a = 0.5 * (xbuf[i, g, rows(c), :].astype(F32) + kbuf[i, g, rows(c), :].astype(F32)) + time_vec
            if g == 0:
                a = a + cond[...]
            a_scr[c, g * part:(g + 1) * part, :] = a
        a = a_scr[c]
        normed = (a * lax.rsqrt(jnp.mean(a * a, axis=-1, keepdims=True) + 1e-6)).astype(BF16)
        tile = 256 if hidden % 256 == 0 else hidden
        for j in range(0, hidden, tile):
            gate = jnp.dot(normed, w_in[:, hidden + j:hidden + j + tile], preferred_element_type=F32)
            value = jnp.dot(normed, w_in[:, j:j + tile], preferred_element_type=F32)
            gelu = 0.5 * gate * (1.0 + lax.erf(gate * math.sqrt(0.5)))
            h_scr[c, :, j:j + tile] = (value * gelu).astype(BF16)

    def back(i, c):
        out = (a_scr[c] + jnp.dot(h_scr[c], w_all[...], preferred_element_type=F32)).astype(BF16)

        @pl.when(i < steps - 1)
        def _():
            ybuf[i + 1, :, rows(c), :] = out.reshape(2, part, channels)

            @pl.when(s < last)
            def _():
                x_copy(ybuf.at[i + 1, :, rows(c), :], i + 1, c).start()
            k_copy(ybuf.at[i + 1, :, rows(c), :], i + 1, c).start()

        @pl.when(i == steps - 1)
        def _():
            oseg_ref[:, rows(c), :] = out.reshape(2, part, channels)

        @pl.when(s == last)
        def _():
            v = out.astype(F32)
            v = v * lax.rsqrt(jnp.mean(v * v, axis=-1, keepdims=True) + 1e-6)
            m = (v * (1.0 / (1.0 + jnp.exp(-v)))).astype(BF16)
            e = lax.dot_general(m, cout[...].astype(BF16), (((1,), (1,)), ((), ())), preferred_element_type=F32)
            guided = e[part:] + guidance_scale * (e[:part] - e[part:])
            root_now, root_next = roots[pl.ds(i, 1), :], roots[pl.ds(i + 1, 1), :]
            rest_now, rest_next = rests[pl.ds(i, 1), :], rests[pl.ds(i + 1, 1), :]
            clean = (lat[rows(c), :] - rest_now * guided) / root_now
            new = root_next * clean + rest_next * guided
            lat[rows(c), :] = new

            @pl.when(i < steps - 1)
            def _():
                latout[i + 1, rows(c), :] = new.astype(BF16)
                l_copy(i + 1, c).start()

    def pass_on(k):
        @pl.when(z >= k)
        def _():
            b = me - 2 * k
            g_arrived(b)

            @pl.when(z < length - 1)
            def _():
                g_copy(b, me + 2, g_line.at[0]).start()
            g_copy(b, side, g_side).start()

        @pl.when(z + k < length)
        def _():
            b = me + 2 * k
            g_arrived(b)

            @pl.when(z > 0)
            def _():
                g_copy(b, me - 2, g_line.at[1]).start()
            g_copy(b, side, g_side).start()

    if not gathered:
        pass_on(1)
    loads[1].wait()
    for c in range(CHUNKS):
        front(0, c)
    loads[2].wait()
    if not gathered:
        for k in range(2, length):
            pass_on(k)
        for k in range(length):
            g_arrived(2 * k + (1 - y))
    for c in range(CHUNKS):
        back(0, c)

    def body(i, carry):
        for c in range(CHUNKS):
            front(i, c)
            back(i, c)
        return carry

    lax.fori_loop(1, steps, body, 0)

    @pl.when(s == last)
    def _():
        turned = lat[...].T
        here = olat_ref.shape[0]
        for d in range(sects):
            fin[d] = turned[d * here:(d + 1) * here, :]
        for d in range(sects - 1):
            f_copy(d).start()
        olat_ref[...] = fin[last]
        for d in range(sects - 1):
            f_copy(d).wait_send()
        for i in range(1, steps):
            for c in range(CHUNKS):
                l_copy(i, c).wait_send()

    @pl.when(s < last)
    def _():
        f_copy(0).wait_recv()
        olat_ref[...] = fin_in[...]
        for i in range(steps):
            for c in range(CHUNKS):
                x_copy(ybuf.at[i, :, rows(c), :], i, c).wait_send()

    for i in range(steps):
        for c in range(CHUNKS):
            k_copy(ybuf.at[i, :, rows(c), :], i, c).wait_send()
    if not gathered:
        for d in range(1, batches):
            p_copy(d).wait_send()
        for k in range(length):
            @pl.when(z >= k)
            def _(k=k):
                b = me - 2 * k

                @pl.when(z < length - 1)
                def _():
                    g_copy(b, me + 2, g_line.at[0]).wait_send()
                g_copy(b, side, g_side).wait_send()

            @pl.when(z + k < length)
            def _(k=k):
                b = me + 2 * k

                @pl.when(z > 0)
                def _():
                    g_copy(b, me - 2, g_line.at[1]).wait_send()
                if k > 0:
                    g_copy(b, side, g_side).wait_send()


def on_device(
    sects, batches, warm, latents, timesteps, assign, prompts, w_in, time_w, w_out, conv_in_w, conv_out_w
):
    positions = latents.shape[1]
    channels = warm.shape[1]
    hidden = w_out.shape[0] * batches
    steps = timesteps.shape[0] - 1
    gathered = w_out.shape[0] % 16 != 0 or batches % 2 != 0
    if gathered:
        w_out = lax.all_gather(w_out, "batch", axis=0, tiled=True)
        table = lax.all_gather(prompts, "batch", axis=0, tiled=True)
        prompts = lax.dynamic_slice_in_dim(table, assign[0], 1, 0).astype(F32)
    whole = pl.BlockSpec(memory_space=pltpu.VMEM)
    apart = pl.BlockSpec(memory_space=pltpu.HBM)
    here = latents.shape[0] // sects
    dma = pltpu.SemaphoreType.DMA
    width = 2 * positions // CHUNKS
    segment, final = pl.pallas_call(
        functools.partial(kernel, sects, batches, gathered),
        out_shape=(
            jax.ShapeDtypeStruct((2, positions, channels), BF16),
            jax.ShapeDtypeStruct((here, positions), F32),
        ),
        in_specs=[apart] * 10,
        out_specs=(whole, whole),
        scratch_shapes=[
            pltpu.SMEM(timesteps.shape, jnp.int32),
            pltpu.SMEM(assign.shape, jnp.int32),
            pltpu.VMEM(latents.shape, F32),
            pltpu.VMEM(prompts.shape, prompts.dtype),
            pltpu.VMEM(conv_in_w.shape, BF16),
            pltpu.VMEM(conv_out_w.shape, BF16),
            pltpu.VMEM(w_in.shape, BF16),
            pltpu.VMEM(time_w.shape, BF16),
            pltpu.VMEM((hidden, channels), BF16),
            pltpu.VMEM((steps, 2, positions, channels), BF16),
            pltpu.VMEM((steps, 2, positions, channels), BF16),
            pltpu.VMEM((steps, 2, positions, channels), BF16),
            pltpu.VMEM((CHUNKS, width, channels), F32),
            pltpu.VMEM((CHUNKS, width, hidden), BF16),
            pltpu.VMEM((16, channels), F32),
            pltpu.VMEM((16, 128), F32),
            pltpu.VMEM((16, 128), F32),
            pltpu.VMEM((1, channels), F32),
            pltpu.VMEM((batches, 1, channels), F32),
            pltpu.VMEM((1, channels), F32),
            pltpu.VMEM((128, channels), F32),
            pltpu.VMEM((128, channels), F32),
            pltpu.VMEM((128, positions), F32),
            pltpu.VMEM((steps, positions, 128), BF16),
            pltpu.VMEM((steps, positions, 128), BF16),
            pltpu.VMEM((sects, here, positions), F32),
            pltpu.VMEM((here, positions), F32),
            dma((9,)),
            dma((steps, CHUNKS)), dma((steps, CHUNKS)),
            dma((steps, CHUNKS)), dma((steps, CHUNKS)),
            dma((steps, CHUNKS)), dma((steps, CHUNKS)),
            dma((sects,)), dma(()),
            dma((batches,)), dma((batches,)),
            dma((2, batches)), dma((batches,)), dma((batches,)),
        ],
        compiler_params=pltpu.CompilerParams(
            collective_id=0, has_side_effects=True, vmem_limit_bytes=60 * 1024 * 1024
        ),
    )(
        timesteps, assign, warm.reshape(2, positions, channels), latents, prompts,
        w_in, time_w, w_out, conv_in_w, conv_out_w,
    )
    return segment.reshape(2 * positions, channels), final


def solution(mesh):
    return jax.shard_map(
        functools.partial(on_device, mesh.shape["sect"], mesh.shape["batch"]),
        mesh=mesh,
        in_specs=(
            P(("sect", "batch"), None),
            P(None, "batch"),
            P(),
            P("batch"),
            P("batch", None),
            P("sect", None),
            P("sect", None),
            P(("sect", "batch"), None),
            P(),
            P(),
        ),
        out_specs=(P(("sect", "batch"), None), P("sect", "batch")),
        check_vma=False,
    )
```

```python
import functools
import math

import jax
import jax.numpy as jnp
from jax import lax
from jax.experimental import pallas as pl
from jax.experimental.pallas import tpu as pltpu
from jax.sharding import PartitionSpec as P

guidance_scale = 3.0
MESH = pl.DeviceIdType.MESH
F32 = jnp.float32
BF16 = jnp.bfloat16
CHUNKS = 2
SPLIT = (384, 256)


def column_pieces(channels):
    widths = SPLIT if sum(SPLIT) == channels else (channels,)
    return [(sum(widths[:j]), width) for j, width in enumerate(widths)]


def kernel(
    sects, batches, gathered,
    ts_hbm, assign_hbm, warm_ref, lat_hbm, prompts_hbm, w_in_ref, time_w_ref, w_out_ref, cin_hbm, cout_hbm,
    oseg_ref, olat_ref,
    ts_ref, assign_ref, lat_ref, prompts_ref, cin_ref, cout_ref,
    w_in, time_w, w_all, xbuf, kbuf, ybuf, a_scr, h_scr, tv, roots, rests, cond, ptab, pown,
    cin, cout, lat, latin, latout, fin, fin_in,
    load_sem, x_send, x_recv, k_send, k_recv, l_send, l_recv, f_send, f_recv,
    p_send, p_recv, g_line, g_side, g_recv, xc_send, xc_recv, kc_send, kc_recv,
):
    s = lax.axis_index("sect")
    me = lax.axis_index("batch")
    steps = ts_ref.shape[0] - 1
    _, positions, channels = warm_ref.shape
    hidden = w_all.shape[0]
    part = positions // CHUNKS
    up = lax.rem(s + 1, sects)
    down = lax.rem(s + sects - 1, sects)
    last = sects - 1
    pieces = column_pieces(channels)
    final_piece = len(pieces) - 1

    loads = [
        pltpu.make_async_copy(time_w_ref, time_w, load_sem.at[0]),
        pltpu.make_async_copy(w_in_ref, w_in, load_sem.at[1]),
    ]
    if gathered:
        loads.append(pltpu.make_async_copy(w_out_ref, w_all, load_sem.at[2]))
    else:
        depth = w_out_ref.shape[0]
        own_rows = pl.ds(pl.multiple_of(me * depth, depth), depth)
        loads.append(pltpu.make_async_copy(w_out_ref, w_all.at[own_rows], load_sem.at[2]))
    pairs = [(prompts_hbm, prompts_ref), (ts_hbm, ts_ref), (assign_hbm, assign_ref), (lat_hbm, lat_ref),
             (cin_hbm, cin_ref), (cout_hbm, cout_ref)]
    for j, (src, dst) in enumerate(pairs):
        loads.append(pltpu.make_async_copy(src, dst, load_sem.at[3 + j]))
    for copy in loads[3:] + loads[:3]:
        copy.start()

    barrier = pltpu.get_barrier_semaphore()
    for d in range(1, sects):
        pl.semaphore_signal(barrier, inc=1, device_id={"sect": lax.rem(s + d, sects)}, device_id_type=MESH)
    met = sects - 1
    if not gathered:
        for d in range(1, batches):
            pl.semaphore_signal(barrier, inc=1, device_id={"batch": lax.rem(me + d, batches)}, device_id_type=MESH)
        met += batches - 1
        loads[3].wait()
        pown[...] = prompts_ref[...].astype(F32)
    pl.semaphore_wait(barrier, met)

    def rows(c):
        return pl.ds(c * part, part)

    def x_copy(src, slot, c):
        return pltpu.make_async_remote_copy(
            src_ref=src, dst_ref=xbuf.at[slot, :, rows(c), :], send_sem=x_send.at[slot, c],
            recv_sem=x_recv.at[slot, c], device_id={"sect": up}, device_id_type=MESH)

    def k_copy(src, slot, c):
        return pltpu.make_async_remote_copy(
            src_ref=src, dst_ref=kbuf.at[slot, :, rows(c), :], send_sem=k_send.at[slot, c],
            recv_sem=k_recv.at[slot, c], device_id={"sect": down}, device_id_type=MESH)

    def columns(ref, j, c=None):
        at, width = pieces[j]
        return ref.at[1, :, slice(None) if c is None else rows(c), pl.ds(at, width)]

    def x_part(j, c=None):
        sems = (xc_send.at[j], xc_recv.at[j]) if c is None else (x_send.at[1, c], x_recv.at[1, c])
        return pltpu.make_async_remote_copy(
            src_ref=columns(ybuf, j, c), dst_ref=columns(xbuf, j, c), send_sem=sems[0],
            recv_sem=sems[1], device_id={"sect": up}, device_id_type=MESH)

    def k_part(j, c=None):
        sems = (kc_send.at[j], kc_recv.at[j]) if c is None else (k_send.at[1, c], k_recv.at[1, c])
        return pltpu.make_async_remote_copy(
            src_ref=columns(ybuf, j, c), dst_ref=columns(kbuf, j, c), send_sem=sems[0],
            recv_sem=sems[1], device_id={"sect": down}, device_id_type=MESH)

    def l_copy(slot, c):
        return pltpu.make_async_remote_copy(
            src_ref=latout.at[slot, rows(c), :], dst_ref=latin.at[slot, rows(c), :], send_sem=l_send.at[slot, c],
            recv_sem=l_recv.at[slot, c], device_id={"sect": 0}, device_id_type=MESH)

    def f_copy(d):
        return pltpu.make_async_remote_copy(
            src_ref=fin.at[d], dst_ref=fin_in, send_sem=f_send.at[d],
            recv_sem=f_recv, device_id={"sect": d}, device_id_type=MESH)

    if not gathered:
        z, y = me // 2, lax.rem(me, 2)
        length = batches // 2
        side = z * 2 + (1 - y)

        def p_copy(d):
            return pltpu.make_async_remote_copy(
                src_ref=pown, dst_ref=ptab.at[me], send_sem=p_send.at[d], recv_sem=p_recv.at[me],
                device_id={"batch": lax.rem(me + d, batches)}, device_id_type=MESH)

        def block(j, b):
            at, width = pieces[j]
            return w_all.at[pl.ds(pl.multiple_of(b * depth, depth), depth), pl.ds(at, width)]

        def g_copy(j, b, to, sem, own=False):
            at, width = pieces[j]
            return pltpu.make_async_remote_copy(
                src_ref=w_out_ref.at[:, pl.ds(at, width)] if own else block(j, b), dst_ref=block(j, b), send_sem=sem,
                recv_sem=g_recv.at[j, b], device_id={"batch": to}, device_id_type=MESH)

        def g_up(j, b, own=False):
            return g_copy(j, b, me + 2, g_line.at[0, j, b], own)

        def g_down(j, b, own=False):
            return g_copy(j, b, me - 2, g_line.at[1, j, b], own)

        def g_side_copy(j, b, own=False):
            return g_copy(j, b, side, g_side.at[j, b], own)

        def g_arrived(j, b):
            pltpu.make_async_copy(block(j, b), block(j, b), g_recv.at[j, b]).wait()

        middle = 1 if len(pieces) > 1 else -1

        def own(j, act):
            @pl.when(z < length - 1)
            def _():
                act(g_up(j, me, True))

            @pl.when(z > 0)
            def _():
                act(g_down(j, me, True))
            act(g_side_copy(j, me, True))

        def pass_on(j, k, act, arrive):
            @pl.when(z >= k)
            def _():
                b = me - 2 * k
                if arrive:
                    g_arrived(j, b)

                @pl.when(z < length - 1)
                def _():
                    act(g_up(j, b))
                if not (j == middle and k == 1):
                    act(g_side_copy(j, b))

            @pl.when(z + k < length)
            def _():
                b = me + 2 * k
                if arrive:
                    g_arrived(j, b)

                @pl.when(z > 0)
                def _():
                    act(g_down(j, b))
                if j == middle and k == 1:
                    @pl.when(z > 0)
                    def _():
                        act(g_side_copy(j, b))
                else:
                    act(g_side_copy(j, b))

        def extra(act, arrive):
            if arrive:
                g_arrived(middle, side)

            @pl.when(z < length - 1)
            def _():
                act(g_up(middle, side))

            @pl.when(z == 1)
            def _():
                act(g_down(middle, side))

        def start(copy):
            copy.start()

        def sent(copy):
            copy.wait_send()

        def piece_here(j):
            for k in range(length):
                b = 2 * k + (1 - y)
                if j == middle:
                    @pl.when(b != side)
                    def _():
                        g_arrived(j, b)
                else:
                    g_arrived(j, b)

        for d in range(1, batches):
            p_copy(d).start()
        own(0, start)
        if final_piece > 0:
            own(1, start)

    for c in range(CHUNKS):
        @pl.when(s < last)
        def _(c=c):
            x_copy(warm_ref.at[:, rows(c), :], 0, c).start()
        k_copy(warm_ref.at[:, rows(c), :], 0, c).start()

    if gathered:
        loads[3].wait()
    for copy in loads[4:]:
        copy.wait()
    cin[...] = jnp.zeros_like(cin)
    cout[...] = jnp.zeros_like(cout)
    levels = cin_ref.shape[0]
    cin[0:levels, :] = cin_ref[...].astype(F32)
    cout[0:levels, :] = cout_ref[...].astype(F32)
    lat[...] = jnp.zeros_like(lat)
    lat[0:levels, :] = lat_ref[...]
    turned = lat[...].T
    lat[...] = turned
    latin[0] = turned.astype(BF16)
    which = lax.broadcasted_iota(jnp.int32, (16, 128), 0)
    times = jnp.zeros((16, 128), F32)
    for i in range(steps + 1):
        times = jnp.where(which == i, ts_ref[i].astype(F32), times)
    bar = jnp.cos((times / 1000.0 + 0.008) / 1.008 * (math.pi / 2)) ** 2
    roots[...] = jnp.sqrt(bar)
    rests[...] = jnp.sqrt(1.0 - bar)
    half = channels // 2
    lane = lax.broadcasted_iota(jnp.int32, (16, channels), 1)
    wave = jnp.where(lane < half, lane, lane - half).astype(F32)
    frequency = jnp.exp(-math.log(10000.0) * wave / half)
    angles = jnp.concatenate([times] * (channels // 128), axis=1) * frequency
    waves = jnp.where(lane < half, jnp.cos(angles), jnp.sin(angles))
    embedded = (waves * (1.0 / (1.0 + jnp.exp(-waves)))).astype(BF16)
    loads[0].wait()
    tv[...] = jnp.dot(embedded, time_w[...], preferred_element_type=F32)

    if gathered:
        cond[...] = prompts_ref[...]
    else:
        ptab[me] = pown[...]
        for d in range(1, batches):
            b = lax.rem(me + d, batches)
            pltpu.make_async_copy(ptab.at[b], ptab.at[b], p_recv.at[b]).wait()
        cond[...] = ptab[assign_ref[0]]

    def front(i, c, parts=False):
        @pl.when(s == 0)
        def _():
            @pl.when(i > 0)
            def _():
                l_copy(i, c).wait_recv()
            first = jnp.dot(latin[i, rows(c), :], cin[...].astype(BF16), preferred_element_type=F32).astype(BF16)
            xbuf[i, 0, rows(c), :] = first
            xbuf[i, 1, rows(c), :] = first

        @pl.when(s > 0)
        def _():
            if parts:
                if c == 0:
                    for j in range(final_piece):
                        x_part(j).wait_recv()
                x_part(final_piece, c).wait_recv()
            else:
                x_copy(ybuf.at[i, :, rows(c), :], i, c).wait_recv()

        if parts:
            if c == 0:
                for j in range(final_piece):
                    k_part(j).wait_recv()
            k_part(final_piece, c).wait_recv()
        else:
            k_copy(ybuf.at[i, :, rows(c), :], i, c).wait_recv()
        time_vec = tv[pl.ds(i, 1), :]
        for g in range(2):
            a = 0.5 * (xbuf[i, g, rows(c), :].astype(F32) + kbuf[i, g, rows(c), :].astype(F32)) + time_vec
            if g == 0:
                a = a + cond[...]
            a_scr[c, g * part:(g + 1) * part, :] = a
        a = a_scr[c]
        normed = (a * lax.rsqrt(jnp.mean(a * a, axis=-1, keepdims=True) + 1e-6)).astype(BF16)
        tile = 256 if hidden % 256 == 0 else hidden
        for j in range(0, hidden, tile):
            gate = jnp.dot(normed, w_in[:, hidden + j:hidden + j + tile], preferred_element_type=F32)
            value = jnp.dot(normed, w_in[:, j:j + tile], preferred_element_type=F32)
            gelu = 0.5 * gate * (1.0 + lax.erf(gate * math.sqrt(0.5)))
            h_scr[c, :, j:j + tile] = (value * gelu).astype(BF16)

    def back(i, c):
        out = (a_scr[c] + jnp.dot(h_scr[c], w_all[...], preferred_element_type=F32)).astype(BF16)

        @pl.when(i < steps - 1)
        def _():
            ybuf[i + 1, :, rows(c), :] = out.reshape(2, part, channels)

            @pl.when(s < last)
            def _():
                x_copy(ybuf.at[i + 1, :, rows(c), :], i + 1, c).start()
            k_copy(ybuf.at[i + 1, :, rows(c), :], i + 1, c).start()

        @pl.when(i == steps - 1)
        def _():
            oseg_ref[:, rows(c), :] = out.reshape(2, part, channels)
        denoise(i, c, out)

    def back_piece(j, c):
        at, width = pieces[j]
        out = a_scr[c, :, at:at + width] + jnp.dot(h_scr[c], w_all[:, at:at + width], preferred_element_type=F32)
        ybuf[1, :, rows(c), at:at + width] = out.astype(BF16).reshape(2, part, width)

    def send_piece(j, c=None):
        @pl.when(s < last)
        def _():
            x_part(j, c).start()
        k_part(j, c).start()

    def denoise(i, c, out):
        @pl.when(s == last)
        def _():
            v = out.astype(F32)
            v = v * lax.rsqrt(jnp.mean(v * v, axis=-1, keepdims=True) + 1e-6)
            m = (v * (1.0 / (1.0 + jnp.exp(-v)))).astype(BF16)
            e = lax.dot_general(m, cout[...].astype(BF16), (((1,), (1,)), ((), ())), preferred_element_type=F32)
            guided = e[part:] + guidance_scale * (e[:part] - e[part:])
            root_now, root_next = roots[pl.ds(i, 1), :], roots[pl.ds(i + 1, 1), :]
            rest_now, rest_next = rests[pl.ds(i, 1), :], rests[pl.ds(i + 1, 1), :]
            clean = (lat[rows(c), :] - rest_now * guided) / root_now
            new = root_next * clean + rest_next * guided
            lat[rows(c), :] = new

            @pl.when(i < steps - 1)
            def _():
                latout[i + 1, rows(c), :] = new.astype(BF16)
                l_copy(i + 1, c).start()

    def back_pieces(j):
        for c in range(CHUNKS):
            back_piece(j, c)
            if j == final_piece:
                send_piece(j, c)
                denoise(0, c, ybuf[1, :, rows(c), :].reshape(2 * part, channels))
        if j < final_piece:
            send_piece(j)

    def fronts(c):
        if c == 0:
            loads[1].wait()
        front(0, c)

    if gathered:
        for c in range(CHUNKS):
            fronts(c)
        loads[2].wait()
        for j in range(len(pieces)):
            back_pieces(j)
    else:
        for k in range(1, length):
            pass_on(0, k, start, True)
        if middle == 1:
            extra(start, True)
            pass_on(1, 1, start, True)
        fronts(0)
        for j in range(2, len(pieces)):
            own(j, start)
        if middle == 1 and length > 2:
            pass_on(1, 2, start, True)
        for c in range(1, CHUNKS):
            fronts(c)
        loads[2].wait()
        for j in range(len(pieces)):
            if j + 1 < len(pieces):
                for k in range(3 if j == 0 else 1, length):
                    pass_on(j + 1, k, start, True)
            piece_here(j)
            back_pieces(j)
    for c in range(CHUNKS):
        front(1, c, True)
        back(1, c)

    def body(i, carry):
        for c in range(CHUNKS):
            front(i, c)
            back(i, c)
        return carry

    lax.fori_loop(2, steps, body, 0)

    @pl.when(s == last)
    def _():
        turned = lat[...].T
        here = olat_ref.shape[0]
        for d in range(sects):
            fin[d] = turned[d * here:(d + 1) * here, :]
        for d in range(sects - 1):
            f_copy(d).start()
        olat_ref[...] = fin[last]
        for d in range(sects - 1):
            f_copy(d).wait_send()
        for i in range(1, steps):
            for c in range(CHUNKS):
                l_copy(i, c).wait_send()

    @pl.when(s < last)
    def _():
        f_copy(0).wait_recv()
        olat_ref[...] = fin_in[...]
        for c in range(CHUNKS):
            for i in range(steps):
                if i == 1:
                    x_part(final_piece, c).wait_send()
                else:
                    x_copy(ybuf.at[i, :, rows(c), :], i, c).wait_send()
        for j in range(final_piece):
            x_part(j).wait_send()

    for c in range(CHUNKS):
        for i in range(steps):
            if i == 1:
                k_part(final_piece, c).wait_send()
            else:
                k_copy(ybuf.at[i, :, rows(c), :], i, c).wait_send()
    for j in range(final_piece):
        k_part(j).wait_send()
    if not gathered:
        for d in range(1, batches):
            p_copy(d).wait_send()
        for j in range(len(pieces)):
            own(j, sent)
            for k in range(1, length):
                pass_on(j, k, sent, False)
        if middle == 1:
            extra(sent, False)


def on_device(
    sects, batches, warm, latents, timesteps, assign, prompts, w_in, time_w, w_out, conv_in_w, conv_out_w
):
    positions = latents.shape[1]
    channels = warm.shape[1]
    hidden = w_out.shape[0] * batches
    steps = timesteps.shape[0] - 1
    gathered = w_out.shape[0] % 16 != 0 or batches % 2 != 0
    if gathered:
        w_out = lax.all_gather(w_out, "batch", axis=0, tiled=True)
        table = lax.all_gather(prompts, "batch", axis=0, tiled=True)
        prompts = lax.dynamic_slice_in_dim(table, assign[0], 1, 0).astype(F32)
    whole = pl.BlockSpec(memory_space=pltpu.VMEM)
    apart = pl.BlockSpec(memory_space=pltpu.HBM)
    here = latents.shape[0] // sects
    pieces = len(column_pieces(channels))
    dma = pltpu.SemaphoreType.DMA
    width = 2 * positions // CHUNKS
    segment, final = pl.pallas_call(
        functools.partial(kernel, sects, batches, gathered),
        out_shape=(
            jax.ShapeDtypeStruct((2, positions, channels), BF16),
            jax.ShapeDtypeStruct((here, positions), F32),
        ),
        in_specs=[apart] * 10,
        out_specs=(whole, whole),
        scratch_shapes=[
            pltpu.SMEM(timesteps.shape, jnp.int32),
            pltpu.SMEM(assign.shape, jnp.int32),
            pltpu.VMEM(latents.shape, F32),
            pltpu.VMEM(prompts.shape, prompts.dtype),
            pltpu.VMEM(conv_in_w.shape, BF16),
            pltpu.VMEM(conv_out_w.shape, BF16),
            pltpu.VMEM(w_in.shape, BF16),
            pltpu.VMEM(time_w.shape, BF16),
            pltpu.VMEM((hidden, channels), BF16),
            pltpu.VMEM((steps, 2, positions, channels), BF16),
            pltpu.VMEM((steps, 2, positions, channels), BF16),
            pltpu.VMEM((steps, 2, positions, channels), BF16),
            pltpu.VMEM((CHUNKS, width, channels), F32),
            pltpu.VMEM((CHUNKS, width, hidden), BF16),
            pltpu.VMEM((16, channels), F32),
            pltpu.VMEM((16, 128), F32),
            pltpu.VMEM((16, 128), F32),
            pltpu.VMEM((1, channels), F32),
            pltpu.VMEM((batches, 1, channels), F32),
            pltpu.VMEM((1, channels), F32),
            pltpu.VMEM((128, channels), F32),
            pltpu.VMEM((128, channels), F32),
            pltpu.VMEM((128, positions), F32),
            pltpu.VMEM((steps, positions, 128), BF16),
            pltpu.VMEM((steps, positions, 128), BF16),
            pltpu.VMEM((sects, here, positions), F32),
            pltpu.VMEM((here, positions), F32),
            dma((9,)),
            dma((steps, CHUNKS)), dma((steps, CHUNKS)),
            dma((steps, CHUNKS)), dma((steps, CHUNKS)),
            dma((steps, CHUNKS)), dma((steps, CHUNKS)),
            dma((sects,)), dma(()),
            dma((batches,)), dma((batches,)),
            dma((2, pieces, batches)), dma((pieces, batches)), dma((pieces, batches)),
            dma((pieces,)), dma((pieces,)), dma((pieces,)), dma((pieces,)),
        ],
        compiler_params=pltpu.CompilerParams(
            collective_id=0, has_side_effects=True, vmem_limit_bytes=60 * 1024 * 1024
        ),
    )(
        timesteps, assign, warm.reshape(2, positions, channels), latents, prompts,
        w_in, time_w, w_out, conv_in_w, conv_out_w,
    )
    return segment.reshape(2 * positions, channels), final


def solution(mesh):
    return jax.shard_map(
        functools.partial(on_device, mesh.shape["sect"], mesh.shape["batch"]),
        mesh=mesh,
        in_specs=(
            P(("sect", "batch"), None),
            P(None, "batch"),
            P(),
            P("batch"),
            P("batch", None),
            P("sect", None),
            P("sect", None),
            P(("sect", "batch"), None),
            P(),
            P(),
        ),
        out_specs=(P(("sect", "batch"), None), P("sect", "batch")),
        check_vma=False,
    )
```

```python
import functools
import math

import jax
import jax.numpy as jnp
from jax import lax
from jax.experimental import pallas as pl
from jax.experimental.pallas import tpu as pltpu
from jax.sharding import PartitionSpec as P

guidance_scale = 3.0
MESH = pl.DeviceIdType.MESH
F32 = jnp.float32
BF16 = jnp.bfloat16
CHUNKS = 2
SPLIT = (512, 128)


def column_pieces(channels):
    widths = SPLIT if sum(SPLIT) == channels else (channels,)
    return [(sum(widths[:j]), width) for j, width in enumerate(widths)]


def kernel(
    sects, batches, gathered,
    ts_hbm, assign_hbm, warm_ref, lat_hbm, prompts_hbm, w_in_ref, time_w_ref, w_out_ref, cin_hbm, cout_hbm,
    oseg_ref, olat_ref,
    ts_ref, assign_ref, lat_ref, prompts_ref, cin_ref, cout_ref,
    w_in, time_w, w_all, xbuf, kbuf, ybuf, a_scr, h_scr, tv, roots, rests, cond, ptab, pown,
    cin, cout, lat, latin, latout, fin, fin_in,
    load_sem, x_send, x_recv, k_send, k_recv, l_send, l_recv, f_send, f_recv,
    p_send, p_recv, g_line, g_side, g_recv, xc_send, xc_recv, kc_send, kc_recv,
):
    s = lax.axis_index("sect")
    me = lax.axis_index("batch")
    steps = ts_ref.shape[0] - 1
    _, positions, channels = warm_ref.shape
    hidden = w_all.shape[0]
    part = positions // CHUNKS
    up = lax.rem(s + 1, sects)
    down = lax.rem(s + sects - 1, sects)
    last = sects - 1
    pieces = column_pieces(channels)
    final_piece = len(pieces) - 1

    loads = [
        pltpu.make_async_copy(time_w_ref, time_w, load_sem.at[0]),
        pltpu.make_async_copy(w_in_ref, w_in, load_sem.at[1]),
    ]
    if gathered:
        loads.append(pltpu.make_async_copy(w_out_ref, w_all, load_sem.at[2]))
    else:
        depth = w_out_ref.shape[0]
        own_rows = pl.ds(pl.multiple_of(me * depth, depth), depth)
        loads.append(pltpu.make_async_copy(w_out_ref, w_all.at[own_rows], load_sem.at[2]))
    pairs = [(prompts_hbm, prompts_ref), (ts_hbm, ts_ref), (assign_hbm, assign_ref), (lat_hbm, lat_ref),
             (cin_hbm, cin_ref), (cout_hbm, cout_ref)]
    for j, (src, dst) in enumerate(pairs):
        loads.append(pltpu.make_async_copy(src, dst, load_sem.at[3 + j]))
    for copy in loads[3:] + loads[:3]:
        copy.start()

    barrier = pltpu.get_barrier_semaphore()
    for d in range(1, sects):
        pl.semaphore_signal(barrier, inc=1, device_id={"sect": lax.rem(s + d, sects)}, device_id_type=MESH)
    met = sects - 1
    if not gathered:
        for d in range(1, batches):
            pl.semaphore_signal(barrier, inc=1, device_id={"batch": lax.rem(me + d, batches)}, device_id_type=MESH)
        met += batches - 1
        loads[3].wait()
        pown[...] = prompts_ref[...].astype(F32)
    pl.semaphore_wait(barrier, met)

    def rows(c):
        return pl.ds(c * part, part)

    def x_copy(src, slot, c):
        return pltpu.make_async_remote_copy(
            src_ref=src, dst_ref=xbuf.at[slot, :, rows(c), :], send_sem=x_send.at[slot, c],
            recv_sem=x_recv.at[slot, c], device_id={"sect": up}, device_id_type=MESH)

    def k_copy(src, slot, c):
        return pltpu.make_async_remote_copy(
            src_ref=src, dst_ref=kbuf.at[slot, :, rows(c), :], send_sem=k_send.at[slot, c],
            recv_sem=k_recv.at[slot, c], device_id={"sect": down}, device_id_type=MESH)

    def columns(ref, j, c=None):
        at, width = pieces[j]
        return ref.at[1, :, slice(None) if c is None else rows(c), pl.ds(at, width)]

    def x_part(j, c=None):
        sems = (xc_send.at[j], xc_recv.at[j]) if c is None else (x_send.at[1, c], x_recv.at[1, c])
        return pltpu.make_async_remote_copy(
            src_ref=columns(ybuf, j, c), dst_ref=columns(xbuf, j, c), send_sem=sems[0],
            recv_sem=sems[1], device_id={"sect": up}, device_id_type=MESH)

    def k_part(j, c=None):
        sems = (kc_send.at[j], kc_recv.at[j]) if c is None else (k_send.at[1, c], k_recv.at[1, c])
        return pltpu.make_async_remote_copy(
            src_ref=columns(ybuf, j, c), dst_ref=columns(kbuf, j, c), send_sem=sems[0],
            recv_sem=sems[1], device_id={"sect": down}, device_id_type=MESH)

    def l_copy(slot, c):
        return pltpu.make_async_remote_copy(
            src_ref=latout.at[slot, rows(c), :], dst_ref=latin.at[slot, rows(c), :], send_sem=l_send.at[slot, c],
            recv_sem=l_recv.at[slot, c], device_id={"sect": 0}, device_id_type=MESH)

    def f_copy(d):
        return pltpu.make_async_remote_copy(
            src_ref=fin.at[d], dst_ref=fin_in, send_sem=f_send.at[d],
            recv_sem=f_recv, device_id={"sect": d}, device_id_type=MESH)

    if not gathered:
        z, y = me // 2, lax.rem(me, 2)
        length = batches // 2
        side = z * 2 + (1 - y)

        def p_copy(d):
            return pltpu.make_async_remote_copy(
                src_ref=pown, dst_ref=ptab.at[me], send_sem=p_send.at[d], recv_sem=p_recv.at[me],
                device_id={"batch": lax.rem(me + d, batches)}, device_id_type=MESH)

        def block(j, b):
            at, width = pieces[j]
            return w_all.at[pl.ds(pl.multiple_of(b * depth, depth), depth), pl.ds(at, width)]

        def g_copy(j, b, to, sem, own=False):
            at, width = pieces[j]
            return pltpu.make_async_remote_copy(
                src_ref=w_out_ref.at[:, pl.ds(at, width)] if own else block(j, b), dst_ref=block(j, b), send_sem=sem,
                recv_sem=g_recv.at[j, b], device_id={"batch": to}, device_id_type=MESH)

        def g_up(j, b, own=False):
            return g_copy(j, b, me + 2, g_line.at[0, j, b], own)

        def g_down(j, b, own=False):
            return g_copy(j, b, me - 2, g_line.at[1, j, b], own)

        def g_side_copy(j, b, own=False):
            return g_copy(j, b, side, g_side.at[j, b], own)

        def g_arrived(j, b):
            pltpu.make_async_copy(block(j, b), block(j, b), g_recv.at[j, b]).wait()

        middle = 1 if len(pieces) > 1 else -1

        def own(j, act):
            @pl.when(z < length - 1)
            def _():
                act(g_up(j, me, True))

            @pl.when(z > 0)
            def _():
                act(g_down(j, me, True))
            act(g_side_copy(j, me, True))

        def pass_on(j, k, act, arrive):
            @pl.when(z >= k)
            def _():
                b = me - 2 * k
                if arrive:
                    g_arrived(j, b)

                @pl.when(z < length - 1)
                def _():
                    act(g_up(j, b))
                if not (j == middle and k == 1):
                    act(g_side_copy(j, b))

            @pl.when(z + k < length)
            def _():
                b = me + 2 * k
                if arrive:
                    g_arrived(j, b)

                @pl.when(z > 0)
                def _():
                    act(g_down(j, b))
                if j == middle and k == 1:
                    @pl.when(z > 0)
                    def _():
                        act(g_side_copy(j, b))
                else:
                    act(g_side_copy(j, b))

        def extra(act, arrive):
            if arrive:
                g_arrived(middle, side)

            @pl.when(z < length - 1)
            def _():
                act(g_up(middle, side))

            @pl.when(z == 1)
            def _():
                act(g_down(middle, side))

        def start(copy):
            copy.start()

        def sent(copy):
            copy.wait_send()

        def piece_here(j):
            for k in range(length):
                b = 2 * k + (1 - y)
                if j == middle:
                    @pl.when(b != side)
                    def _():
                        g_arrived(j, b)
                else:
                    g_arrived(j, b)

        for d in range(1, batches):
            p_copy(d).start()
        own(0, start)
        if final_piece > 0:
            own(1, start)

    for c in range(CHUNKS):
        @pl.when(s < last)
        def _(c=c):
            x_copy(warm_ref.at[:, rows(c), :], 0, c).start()
        k_copy(warm_ref.at[:, rows(c), :], 0, c).start()

    if gathered:
        loads[3].wait()
    for copy in loads[4:]:
        copy.wait()
    cin[...] = jnp.zeros_like(cin)
    cout[...] = jnp.zeros_like(cout)
    levels = cin_ref.shape[0]
    cin[0:levels, :] = cin_ref[...].astype(F32)
    cout[0:levels, :] = cout_ref[...].astype(F32)
    lat[...] = jnp.zeros_like(lat)
    lat[0:levels, :] = lat_ref[...]
    turned = lat[...].T
    lat[...] = turned
    latin[0] = turned.astype(BF16)
    which = lax.broadcasted_iota(jnp.int32, (16, 128), 0)
    times = jnp.zeros((16, 128), F32)
    for i in range(steps + 1):
        times = jnp.where(which == i, ts_ref[i].astype(F32), times)
    bar = jnp.cos((times / 1000.0 + 0.008) / 1.008 * (math.pi / 2)) ** 2
    roots[...] = jnp.sqrt(bar)
    rests[...] = jnp.sqrt(1.0 - bar)
    half = channels // 2
    lane = lax.broadcasted_iota(jnp.int32, (16, channels), 1)
    wave = jnp.where(lane < half, lane, lane - half).astype(F32)
    frequency = jnp.exp(-math.log(10000.0) * wave / half)
    angles = jnp.concatenate([times] * (channels // 128), axis=1) * frequency
    waves = jnp.where(lane < half, jnp.cos(angles), jnp.sin(angles))
    embedded = (waves * (1.0 / (1.0 + jnp.exp(-waves)))).astype(BF16)
    loads[0].wait()
    tv[...] = jnp.dot(embedded, time_w[...], preferred_element_type=F32)

    if gathered:
        cond[...] = prompts_ref[...]
    else:
        ptab[me] = pown[...]
        for d in range(1, batches):
            b = lax.rem(me + d, batches)
            pltpu.make_async_copy(ptab.at[b], ptab.at[b], p_recv.at[b]).wait()
        cond[...] = ptab[assign_ref[0]]

    def front(i, c, parts=False):
        @pl.when(s == 0)
        def _():
            @pl.when(i > 0)
            def _():
                l_copy(i, c).wait_recv()
            first = jnp.dot(latin[i, rows(c), :], cin[...].astype(BF16), preferred_element_type=F32).astype(BF16)
            xbuf[i, 0, rows(c), :] = first
            xbuf[i, 1, rows(c), :] = first

        @pl.when(s > 0)
        def _():
            if parts:
                if c == 0:
                    for j in range(final_piece):
                        x_part(j).wait_recv()
                x_part(final_piece, c).wait_recv()
            else:
                x_copy(ybuf.at[i, :, rows(c), :], i, c).wait_recv()

        if parts:
            if c == 0:
                for j in range(final_piece):
                    k_part(j).wait_recv()
            k_part(final_piece, c).wait_recv()
        else:
            k_copy(ybuf.at[i, :, rows(c), :], i, c).wait_recv()
        time_vec = tv[pl.ds(i, 1), :]
        for g in range(2):
            a = 0.5 * (xbuf[i, g, rows(c), :].astype(F32) + kbuf[i, g, rows(c), :].astype(F32)) + time_vec
            if g == 0:
                a = a + cond[...]
            a_scr[c, g * part:(g + 1) * part, :] = a
        a = a_scr[c]
        normed = (a * lax.rsqrt(jnp.mean(a * a, axis=-1, keepdims=True) + 1e-6)).astype(BF16)
        tile = 256 if hidden % 256 == 0 else hidden
        for j in range(0, hidden, tile):
            gate = jnp.dot(normed, w_in[:, hidden + j:hidden + j + tile], preferred_element_type=F32)
            value = jnp.dot(normed, w_in[:, j:j + tile], preferred_element_type=F32)
            gelu = 0.5 * gate * (1.0 + lax.erf(gate * math.sqrt(0.5)))
            h_scr[c, :, j:j + tile] = (value * gelu).astype(BF16)

    def back(i, c):
        out = (a_scr[c] + jnp.dot(h_scr[c], w_all[...], preferred_element_type=F32)).astype(BF16)

        @pl.when(i < steps - 1)
        def _():
            ybuf[i + 1, :, rows(c), :] = out.reshape(2, part, channels)

            @pl.when(s < last)
            def _():
                x_copy(ybuf.at[i + 1, :, rows(c), :], i + 1, c).start()
            k_copy(ybuf.at[i + 1, :, rows(c), :], i + 1, c).start()

        @pl.when(i == steps - 1)
        def _():
            oseg_ref[:, rows(c), :] = out.reshape(2, part, channels)
        denoise(i, c, out)

    def back_piece(j, c):
        at, width = pieces[j]
        out = a_scr[c, :, at:at + width] + jnp.dot(h_scr[c], w_all[:, at:at + width], preferred_element_type=F32)
        ybuf[1, :, rows(c), at:at + width] = out.astype(BF16).reshape(2, part, width)

    def send_piece(j, c=None):
        @pl.when(s < last)
        def _():
            x_part(j, c).start()
        k_part(j, c).start()

    def denoise(i, c, out):
        @pl.when(s == last)
        def _():
            v = out.astype(F32)
            v = v * lax.rsqrt(jnp.mean(v * v, axis=-1, keepdims=True) + 1e-6)
            m = (v * (1.0 / (1.0 + jnp.exp(-v)))).astype(BF16)
            e = lax.dot_general(m, cout[...].astype(BF16), (((1,), (1,)), ((), ())), preferred_element_type=F32)
            guided = e[part:] + guidance_scale * (e[:part] - e[part:])
            root_now, root_next = roots[pl.ds(i, 1), :], roots[pl.ds(i + 1, 1), :]
            rest_now, rest_next = rests[pl.ds(i, 1), :], rests[pl.ds(i + 1, 1), :]
            clean = (lat[rows(c), :] - rest_now * guided) / root_now
            new = root_next * clean + rest_next * guided
            lat[rows(c), :] = new

            @pl.when(i < steps - 1)
            def _():
                latout[i + 1, rows(c), :] = new.astype(BF16)
                l_copy(i + 1, c).start()

    def back_pieces(j):
        for c in range(CHUNKS):
            back_piece(j, c)
            if j == final_piece:
                send_piece(j, c)
                denoise(0, c, ybuf[1, :, rows(c), :].reshape(2 * part, channels))
        if j < final_piece:
            send_piece(j)

    def fronts(c):
        if c == 0:
            loads[1].wait()
        front(0, c)

    if gathered:
        for c in range(CHUNKS):
            fronts(c)
        loads[2].wait()
        for j in range(len(pieces)):
            back_pieces(j)
    else:
        for k in range(1, length):
            pass_on(0, k, start, True)
        if middle == 1:
            extra(start, True)
            pass_on(1, 1, start, True)
        fronts(0)
        for j in range(2, len(pieces)):
            own(j, start)
        if middle == 1 and length > 2:
            pass_on(1, 2, start, True)
        for c in range(1, CHUNKS):
            fronts(c)
        loads[2].wait()
        for j in range(len(pieces)):
            if j + 1 < len(pieces):
                for k in range(3 if j == 0 else 1, length):
                    pass_on(j + 1, k, start, True)
            piece_here(j)
            back_pieces(j)
    for c in range(CHUNKS):
        front(1, c, True)
        back(1, c)

    def body(i, carry):
        for c in range(CHUNKS):
            front(i, c)
            back(i, c)
        return carry

    lax.fori_loop(2, steps, body, 0)

    @pl.when(s == last)
    def _():
        turned = lat[...].T
        here = olat_ref.shape[0]
        for d in range(sects):
            fin[d] = turned[d * here:(d + 1) * here, :]
        for d in range(sects - 1):
            f_copy(d).start()
        olat_ref[...] = fin[last]
        for d in range(sects - 1):
            f_copy(d).wait_send()
        for i in range(1, steps):
            for c in range(CHUNKS):
                l_copy(i, c).wait_send()

    @pl.when(s < last)
    def _():
        f_copy(0).wait_recv()
        olat_ref[...] = fin_in[...]
        for c in range(CHUNKS):
            for i in range(steps):
                if i == 1:
                    x_part(final_piece, c).wait_send()
                else:
                    x_copy(ybuf.at[i, :, rows(c), :], i, c).wait_send()
        for j in range(final_piece):
            x_part(j).wait_send()

    for c in range(CHUNKS):
        for i in range(steps):
            if i == 1:
                k_part(final_piece, c).wait_send()
            else:
                k_copy(ybuf.at[i, :, rows(c), :], i, c).wait_send()
    for j in range(final_piece):
        k_part(j).wait_send()
    if not gathered:
        for d in range(1, batches):
            p_copy(d).wait_send()
        for j in range(len(pieces)):
            own(j, sent)
            for k in range(1, length):
                pass_on(j, k, sent, False)
        if middle == 1:
            extra(sent, False)


def on_device(
    sects, batches, warm, latents, timesteps, assign, prompts, w_in, time_w, w_out, conv_in_w, conv_out_w
):
    positions = latents.shape[1]
    channels = warm.shape[1]
    hidden = w_out.shape[0] * batches
    steps = timesteps.shape[0] - 1
    gathered = w_out.shape[0] % 16 != 0 or batches % 2 != 0
    if gathered:
        w_out = lax.all_gather(w_out, "batch", axis=0, tiled=True)
        table = lax.all_gather(prompts, "batch", axis=0, tiled=True)
        prompts = lax.dynamic_slice_in_dim(table, assign[0], 1, 0).astype(F32)
    whole = pl.BlockSpec(memory_space=pltpu.VMEM)
    apart = pl.BlockSpec(memory_space=pltpu.HBM)
    here = latents.shape[0] // sects
    pieces = len(column_pieces(channels))
    dma = pltpu.SemaphoreType.DMA
    width = 2 * positions // CHUNKS
    segment, final = pl.pallas_call(
        functools.partial(kernel, sects, batches, gathered),
        out_shape=(
            jax.ShapeDtypeStruct((2, positions, channels), BF16),
            jax.ShapeDtypeStruct((here, positions), F32),
        ),
        in_specs=[apart] * 10,
        out_specs=(whole, whole),
        scratch_shapes=[
            pltpu.SMEM(timesteps.shape, jnp.int32),
            pltpu.SMEM(assign.shape, jnp.int32),
            pltpu.VMEM(latents.shape, F32),
            pltpu.VMEM(prompts.shape, prompts.dtype),
            pltpu.VMEM(conv_in_w.shape, BF16),
            pltpu.VMEM(conv_out_w.shape, BF16),
            pltpu.VMEM(w_in.shape, BF16),
            pltpu.VMEM(time_w.shape, BF16),
            pltpu.VMEM((hidden, channels), BF16),
            pltpu.VMEM((steps, 2, positions, channels), BF16),
            pltpu.VMEM((steps, 2, positions, channels), BF16),
            pltpu.VMEM((steps, 2, positions, channels), BF16),
            pltpu.VMEM((CHUNKS, width, channels), F32),
            pltpu.VMEM((CHUNKS, width, hidden), BF16),
            pltpu.VMEM((16, channels), F32),
            pltpu.VMEM((16, 128), F32),
            pltpu.VMEM((16, 128), F32),
            pltpu.VMEM((1, channels), F32),
            pltpu.VMEM((batches, 1, channels), F32),
            pltpu.VMEM((1, channels), F32),
            pltpu.VMEM((128, channels), F32),
            pltpu.VMEM((128, channels), F32),
            pltpu.VMEM((128, positions), F32),
            pltpu.VMEM((steps, positions, 128), BF16),
            pltpu.VMEM((steps, positions, 128), BF16),
            pltpu.VMEM((sects, here, positions), F32),
            pltpu.VMEM((here, positions), F32),
            dma((9,)),
            dma((steps, CHUNKS)), dma((steps, CHUNKS)),
            dma((steps, CHUNKS)), dma((steps, CHUNKS)),
            dma((steps, CHUNKS)), dma((steps, CHUNKS)),
            dma((sects,)), dma(()),
            dma((batches,)), dma((batches,)),
            dma((2, pieces, batches)), dma((pieces, batches)), dma((pieces, batches)),
            dma((pieces,)), dma((pieces,)), dma((pieces,)), dma((pieces,)),
        ],
        compiler_params=pltpu.CompilerParams(
            collective_id=0, has_side_effects=True, vmem_limit_bytes=60 * 1024 * 1024
        ),
    )(
        timesteps, assign, warm.reshape(2, positions, channels), latents, prompts,
        w_in, time_w, w_out, conv_in_w, conv_out_w,
    )
    return segment.reshape(2 * positions, channels), final


def solution(mesh):
    return jax.shard_map(
        functools.partial(on_device, mesh.shape["sect"], mesh.shape["batch"]),
        mesh=mesh,
        in_specs=(
            P(("sect", "batch"), None),
            P(None, "batch"),
            P(),
            P("batch"),
            P("batch", None),
            P("sect", None),
            P("sect", None),
            P(("sect", "batch"), None),
            P(),
            P(),
        ),
        out_specs=(P(("sect", "batch"), None), P("sect", "batch")),
        check_vma=False,
    )
```
